32 devices in a mesh: dp: 8 (over y, x, core), tensor: 4 (over z).
Axes of the slice: x: 2, y: 2, z: 4, core: 2. Of those that a mesh axis runs over, the one named last changes fastest.
Arguments:
- hidden: bfloat16 [2048, 28672], P('dp', 'tensor'), may hold values from -6 to 6
- hidden_check: bfloat16 [8, 28672], P(None, 'tensor'), may hold values from -96 to 96
- down_weight: bfloat16 [28672, 8192], P('tensor', 'dp'), may hold values from -0.03125 to 0.03125
- weight_check: bfloat16 [28672, 64], P('tensor', 'dp'), may hold values from -0.40039062 to 0.40039062
Outputs:
- output: bfloat16 [2048, 8192], P('tensor', 'dp')
- row_residual: float32 [2048, 64], P('tensor', 'dp')
- col_residual: float32 [8192], P('dp')
The draws below stay inside these ranges and needn't reach their ends.
All inputs are finite; a program needn't handle non-finite values.
Results may differ from the reference program's by a relative error of at most 0.001.
Values may be sent and summed in bfloat16 or wider, within the bound.
No kernel may reach another device: no remote copies, remote signals or barrier semaphores. Data moves between devices by JAX's collectives and lax.ppermute only.
A program may use at most 128 MiB of HBM per device.

```python
import jax
import jax.numpy as jnp

D = 8192
FF = 28672
CHECK_BLOCK = 128
TOK_DEV = 256
TOKENS = 2048
GROUPS = 8


def shard_levels(rng, dims, shards, least, top_value):
    level = 1.0
    for axis_at, parts in shards:
        heights = jax.random.uniform(jax.random.fold_in(jax.random.fold_in(rng, 6), axis_at), (parts,), jnp.float32, least / len(shards), top_value / len(shards))
        level = level * jnp.repeat(jnp.exp(heights), dims[axis_at] // parts).reshape((-1,) + (1,) * (len(dims) - 1 - axis_at))
    return level


def scatter_about(stream_key, extent, scale, most, pieces=(), held_as=jnp.bfloat16):
    gain = shard_levels(stream_key, extent, pieces, -0.22, 0.18) if pieces else 1.0
    values = jax.random.normal(stream_key, extent, jnp.float32) * scale * gain
    return jnp.minimum(jnp.maximum(values, -most), most).astype(held_as)


def setup_inputs(seed: int = 0) -> dict:
    arg_keys = jax.random.split(jax.random.key(seed), 5)
    return {
        "hidden": scatter_about(arg_keys[0], (TOKENS, FF), 1.0, 6.0, ((0, 8), (1, 4))),
        "hidden_check": scatter_about(arg_keys[1], (GROUPS, FF), (TOK_DEV ** 0.5), 96.0, ((1, 4),)),
        "down_weight": scatter_about(arg_keys[2], (FF, D), FF ** -0.5, 0.03125, ((0, 4), (1, 8))),
        "weight_check": scatter_about(arg_keys[3], (FF, D // CHECK_BLOCK), ((CHECK_BLOCK / FF) ** 0.5), 0.40039062, ((0, 4), (1, 8))),
    }


def reference(hidden, hidden_check, down_weight, weight_check):
    product = jnp.dot(hidden, down_weight, preferred_element_type=jnp.float32)
    output = product.astype(jnp.bfloat16)
    check_cols = jnp.dot(hidden, weight_check, preferred_element_type=jnp.float32)
    rows = product.shape[0]
    block_sums = product.reshape(rows, -1, CHECK_BLOCK).sum(-1)
    row_residual = (check_cols - block_sums) * (CHECK_BLOCK ** -0.5)
    check_rows = jnp.dot(hidden_check, down_weight, preferred_element_type=jnp.float32)
    col_residual = (check_rows.sum(0) - product.sum(0)) * (rows ** -0.5)
    return output, row_residual, col_residual
```

```python
import functools

import jax
import jax.numpy as jnp
from jax import lax
from jax.experimental import pallas as pl
from jax.experimental.pallas import tpu as pltpu
from jax.sharding import PartitionSpec as P


CHECK_BLOCK = 128
SPAN = 173.0
TAG = 16
CHUNK = 64
GRANT = 28 * 2**20


def split3(value):
    high = value.astype(jnp.bfloat16)
    rest = value - high.astype(jnp.float32)
    middle = rest.astype(jnp.bfloat16)
    low = (rest - middle.astype(jnp.float32)).astype(jnp.bfloat16)
    return high, middle, low


def across(left, right):
    return lax.dot_general(left, right, (((1,), (1,)), ((), ())), preferred_element_type=jnp.float32)


def multiply_body(index, single, which, first, later, steps, deep, pieces, *refs):
    table, parts, refs = refs[0], refs[1 : 1 + pieces], refs[1 + pieces :]
    if first:
        source, check, stored, *refs = refs
    else:
        weight, check, before, *refs = refs
    if later:
        refs = refs[4:]
    own, send1, send2, send3, differ, column, *refs = refs
    if first:
        weight, *refs = refs
    total, joined, coded, checks, sems, *refs = refs
    if first:
        (arrivals,) = refs
    sends = (send1, send2, send3)
    step = pl.program_id(0)
    rows = differ.shape[2]
    width = total.shape[1]
    blocks = differ.shape[1]
    used = len(which) * rows
    slots = [table[4 * index + b] for b in which]
    places = [b if single else 0 for b in which]

    @pl.when(step == 0)
    def _():
        total[...] = jnp.zeros_like(total)
        checks[...] = jnp.zeros_like(checks)
        if first:
            for i in range(steps):
                at = pl.ds(i * deep, deep)
                pltpu.make_async_copy(source.at[at], weight.at[at], arrivals.at[i]).start()

    at_depth = pl.ds(pl.multiple_of(step * deep, deep), deep)
    place = 0
    for part in parts:
        joined[place : place + part.shape[0]] = part[...]
        place += part.shape[0]
    if first:
        joined[used : used + stored.shape[0]] = stored[...]
    checks[...] += across(check[...], joined[:used])
    if first:
        pltpu.make_async_copy(source.at[at_depth], weight.at[at_depth], arrivals.at[step]).wait()
    total[...] += jnp.dot(joined[...], weight[at_depth, :], preferred_element_type=jnp.float32)

    @pl.when(step == steps - 1)
    def _():
        part = min(CHUNK, rows)
        line = lax.broadcasted_iota(jnp.int32, (blocks, width), 0)
        lane = lax.broadcasted_iota(jnp.int32, (blocks, width), 1)
        member = jnp.where(lane // CHECK_BLOCK == line, 1.0, 0.0).astype(jnp.bfloat16)
        columns = jnp.zeros((1, width), jnp.float32)
        for i, slot in enumerate(slots):
            base = i * rows

            def survey(n, carry):
                summed, largest = carry
                value = total[pl.ds(pl.multiple_of(base + n * part, part), part), :]
                return (
                    summed + value.sum(0, keepdims=True),
                    jnp.maximum(largest, jnp.abs(value).max(0, keepdims=True)),
                )

            zero = jnp.zeros((1, width), jnp.float32)
            summed, largest = lax.fori_loop(0, rows // part, survey, (zero, zero))
            columns += summed
            wide = min(128, rows)
            for n in range(rows // wide):
                at = slice(base + n * wide, base + (n + 1) * wide)
                high, middle, low = split3(total[at, :])
                sums = across(member, high) + across(member, middle) + across(member, low)
                differ[i, :, n * wide : (n + 1) * wide] = checks[:, at] - sums
            scale = (jnp.maximum(largest, 1e-30) * 1.01).astype(jnp.bfloat16)
            per = SPAN / scale.astype(jnp.float32)

            @pl.when(slot != 0)
            def _():
                def encode(n, carry):
                    value = total[pl.ds(pl.multiple_of(base + n * part, part), part), :]
                    size = jnp.exp(jnp.abs(value) * per - SPAN / 2)
                    coded[i, pl.ds(pl.multiple_of(n * part, part), part), :] = jnp.where(
                        value < 0, -size, size
                    ).astype(jnp.bfloat16)
                    return carry

                lax.fori_loop(0, rows // part, encode, 0)
                terms = split3(differ[i])
                if rows < 256:
                    pad = jnp.zeros((blocks, 256 - rows), jnp.bfloat16)
                    terms = [jnp.concatenate([t, pad], 1) for t in terms]
                fill = [*terms, jnp.zeros((blocks, width - 768), jnp.bfloat16)]
                tag = [jnp.concatenate(fill, 1), jnp.broadcast_to(scale, (TAG - blocks, width))]
                coded[i, pl.ds(rows, TAG), :] = jnp.concatenate(tag, 0)

            @pl.when(slot == 0)
            def _():
                pltpu.make_async_copy(total.at[pl.ds(base, rows)], own.at[places[i]], sems.at[i]).start()

            for s in range(3):

                @pl.when(slot == s + 1)
                def _():
                    pltpu.make_async_copy(coded.at[i], sends[s].at[places[i]], sems.at[i]).start()

        if first:
            columns = total[used : used + stored.shape[0], :].sum(0, keepdims=True) - columns
        else:
            columns = before[...] - columns
        column[...] = columns
        for i, slot in enumerate(slots):

            @pl.when(slot == 0)
            def _():
                pltpu.make_async_copy(total.at[pl.ds(i * rows, rows)], own.at[places[i]], sems.at[i]).wait()

            @pl.when(slot != 0)
            def _():
                pltpu.make_async_copy(coded.at[i], send1.at[places[i]], sems.at[i]).wait()


def multiply(table, index, which, parts, weight, check, before, stored, single, earlier):
    parts = [pltpu.with_memory_space_constraint(p, pltpu.HBM) for p in parts]
    rows, depth = sum(p.shape[0] for p in parts) // len(which), parts[0].shape[1]
    width = weight.shape[1]
    blocks = check.shape[0]
    deep = next(d for d in (1792, 1024, 512, 256, 128) if depth % d == 0)
    steps = depth // deep
    count = 2 if single else 1
    first = stored is not None
    thin = pl.BlockSpec((blocks, deep), lambda k, s: (0, k))
    anywhere = pl.BlockSpec(memory_space=pl.ANY)
    inside = pl.BlockSpec(memory_space=pltpu.VMEM)
    in_specs = [pl.BlockSpec((p.shape[0], deep), lambda k, s: (0, k)) for p in parts]
    coded = jax.ShapeDtypeStruct((count, rows + TAG, width), jnp.bfloat16)
    out_specs = [
        anywhere,
        anywhere,
        anywhere,
        anywhere,
        pl.BlockSpec((len(which), blocks, rows), lambda k, s: (0, 0, 0)),
        pl.BlockSpec((1, width), lambda k, s: (0, 0)),
    ]
    out_shape = [
        jax.ShapeDtypeStruct((count, rows, width), jnp.float32),
        coded,
        coded,
        coded,
        jax.ShapeDtypeStruct((len(which), blocks, rows), jnp.float32),
        jax.ShapeDtypeStruct((1, width), jnp.float32),
    ]
    tall = len(which) * rows + (16 if first else 0)
    scratch = [
        pltpu.VMEM((tall, width), jnp.float32),
        pltpu.VMEM((tall, deep), jnp.bfloat16),
        pltpu.VMEM((len(which), rows + TAG, width), jnp.bfloat16),
        pltpu.VMEM((blocks, len(which) * rows), jnp.float32),
        pltpu.SemaphoreType.DMA((2,)),
    ]
    if first:
        in_specs += [anywhere, thin, pl.BlockSpec((stored.shape[0], deep), lambda k, s: (0, k))]
        operands = [table, *parts, weight, check, stored]
        out_specs.append(inside)
        out_shape.append(pltpu.VMEM(weight.shape, weight.dtype))
        scratch.append(pltpu.SemaphoreType.DMA((steps,)))
    else:
        in_specs += [inside, thin, pl.BlockSpec((1, width), lambda k, s: (0, 0))]
        operands = [table, *parts, weight, check, before]
    aliases = {}
    if earlier:
        aliases = {len(operands) + i: i for i in range(4)}
        operands += earlier
        in_specs += [anywhere] * 4
    return pl.pallas_call(
        functools.partial(
            multiply_body, index, single, which, first, bool(earlier), steps, deep, len(parts)
        ),
        grid_spec=pltpu.PrefetchScalarGridSpec(
            num_scalar_prefetch=1,
            grid=(steps,),
            in_specs=in_specs,
            out_specs=out_specs,
            scratch_shapes=scratch,
        ),
        out_shape=out_shape,
        input_output_aliases=aliases,
        cost_estimate=pl.CostEstimate(
            flops=2 * len(which) * rows * depth * width,
            bytes_accessed=2 * len(which) * depth * rows,
            transcendentals=0,
        ),
        compiler_params=pltpu.CompilerParams(
            dimension_semantics=("arbitrary",), vmem_limit_bytes=GRANT
        ),
    )(*operands)


def finish_body(index, single, aliased, *refs):
    table, own, get1, get2, get3, differ, differ2 = refs[:7]
    out, row, held, taken, done, sems = refs[8:] if aliased else refs[7:]
    rows, _ = held.shape
    blocks = differ.shape[1]
    part = min(CHUNK, rows)
    gets = (get1, get2, get3)
    marks = [table[4 * index + i] for i in range(4)]
    row[...] = jnp.zeros_like(row)
    for b in range(2):
        place = b if single else 0

        @pl.when(marks[b] == 0)
        def _():
            copies = [pltpu.make_async_copy(own.at[place], held, sems.at[0])]
            for s in range(3):
                copies.append(pltpu.make_async_copy(gets[s].at[place], taken.at[s], sems.at[s + 1]))
            for copy in copies:
                copy.start()
            for copy in copies:
                copy.wait()
            scales = [taken[s, pl.ds(rows, TAG), :][blocks : blocks + 1].astype(jnp.float32) / SPAN for s in range(3)]

            def decode(i, carry):
                at = pl.ds(pl.multiple_of(i * part, part), part)
                value = held[at, :]
                for s in range(3):
                    code = taken[s, at, :].astype(jnp.float32)
                    size = (jnp.log(jnp.abs(code)) + SPAN / 2) * scales[s]
                    value += jnp.where(code < 0, -size, size)
                done[at, :] = value.astype(jnp.bfloat16)
                return carry

            lax.fori_loop(0, rows // part, decode, 0)
            put = pltpu.make_async_copy(
                done, out.at[pl.ds(pl.multiple_of(marks[2 + b], CHUNK), rows), :], sems.at[0]
            )
            put.start()
            whole = differ2[0] if b else differ[0]
            for s in range(3):
                tag = taken[s, pl.ds(rows, TAG), :][:blocks].astype(jnp.float32)
                for j in range(3):
                    whole += tag[:, j * 256 : j * 256 + rows]
            row[b] = whole
            put.wait()


def finish(table, index, own, gets, differ, out, total_rows, single):
    rows, width = own.shape[1:]
    blocks = differ[0].shape[1]
    anywhere = pl.BlockSpec(memory_space=pl.ANY)
    aliased = out is not None
    operands = [table, own, *gets, differ[0], differ[-1]]
    last = differ[-1].shape[0] - 1
    in_specs = [anywhere] * 4 + [
        pl.BlockSpec((1, blocks, rows), lambda i, s: (0, 0, 0)),
        pl.BlockSpec((1, blocks, rows), lambda i, s: (last, 0, 0)),
    ]
    if aliased:
        operands.append(out)
        in_specs.append(anywhere)
    return pl.pallas_call(
        functools.partial(finish_body, index, single, aliased),
        grid_spec=pltpu.PrefetchScalarGridSpec(
            num_scalar_prefetch=1,
            grid=(1,),
            in_specs=in_specs,
            out_specs=[anywhere, pl.BlockSpec((2, blocks, rows), lambda i, s: (0, 0, 0))],
            scratch_shapes=[
                pltpu.VMEM((rows, width), jnp.float32),
                pltpu.VMEM((3, rows + TAG, width), jnp.bfloat16),
                pltpu.VMEM((rows, width), jnp.bfloat16),
                pltpu.SemaphoreType.DMA((4,)),
            ],
        ),
        out_shape=[
            jax.ShapeDtypeStruct((total_rows, width), jnp.bfloat16),
            jax.ShapeDtypeStruct((2, blocks, rows), jnp.float32),
        ],
        input_output_aliases={7: 0} if aliased else {},
        compiler_params=pltpu.CompilerParams(vmem_limit_bytes=GRANT // 2),
        cost_estimate=pl.CostEstimate(flops=0, bytes_accessed=10 * rows * width, transcendentals=0),
    )(*operands)


def planned(mesh_shape, hidden, hidden_check, down_weight, weight_check):
    lanes, chips = mesh_shape["dp"], mesh_shape["tensor"]
    half = hidden.shape[0]
    total_rows = half * lanes
    cut, quarter = half // 2, half // 4
    plan = (
        ("own", (0,), 0, 0),
        ("0a", (1, 2), 0, 0),
        ("0b", (1, 2), 0, cut),
        ("da", (3,), 1, 0),
        ("db", (3,), 1, cut),
        ("1a", (1, 2), 1, 0),
        ("1b", (1, 2), 1, cut),
        ("1c", (1, 2), 1, cut + quarter),
    )
    me, z = lax.axis_index("dp"), lax.axis_index("tensor")
    core, here = me % 2, (me // 2) ^ z
    entries = []
    for _, kinds, other, at in plan:
        direct, swapped = kinds[0], kinds[-1]
        if direct != swapped:
            direct, swapped = jnp.where(core == 0, direct, swapped), jnp.where(core == 0, swapped, direct)
        side = core ^ other
        entries += [here ^ direct, here ^ swapped, side * half + at, (1 - side) * half + at]
    table = jnp.stack([jnp.asarray(e, jnp.int32) for e in entries])
    check = weight_check.T

    def swap(value):
        return lax.ppermute(value, "dp", [(i, i ^ 1) for i in range(lanes)])

    def mix(value):
        return lax.ppermute(value, "dp", [(i, i ^ (4 if i % 2 else 2)) for i in range(lanes)])

    def along(value, kinds, s):
        pairs = []
        for i in range(lanes):
            for kind in kinds:
                target = (i // 2) ^ kind
                pairs.append((i * chips + (target ^ s), i * chips + target))
        return lax.ppermute(value, ("dp", "tensor"), pairs)

    held = {}
    state = {"out": None, "column": None, "weight": down_weight}

    def group(index, parts, stored=None, which=(0, 1)):
        _, kinds = plan[index][:2]
        single = len(kinds) == 1
        earlier, differ = held.pop(index, (None, []))[:2]
        made = multiply(
            table, index, which, parts, state["weight"], check, state["column"], stored, single, earlier
        )
        sent, more, state["column"] = made[:4], made[4], made[5]
        if stored is not None:
            state["weight"] = pltpu.with_memory_space_constraint(made[6], pltpu.VMEM)
        differ = [*differ, more]
        if which[-1] == 0:
            held[index] = sent, differ
            return
        own, *sends = sent
        gets = [along(v, kinds, s + 1) for s, v in enumerate(sends)]
        held[index] = own, gets, differ, single

    def close(index):
        own, gets, differ, single = held[index]
        state["out"], row = finish(
            table, index, own, gets, differ, state["out"], total_rows // chips, single
        )
        return row

    part_a = hidden[:cut]
    hidden, part_a = lax.optimization_barrier((hidden, part_a))
    part_b = hidden[cut:]
    m0a = mix(part_a)
    pa = swap(part_a)
    m0b = mix(part_b)
    pb = swap(part_b)
    group(0, [part_a, part_b], hidden_check, which=(0,))
    group(0, [pa, pb], which=(1,))
    s0a = swap(m0a)
    d0a = mix(s0a)
    group(1, [m0a, s0a])
    s0b = swap(m0b)
    d0b = mix(s0b)
    m1a = mix(pa)
    m1b = mix(pb[:quarter])
    m1c = mix(pb[quarter:])
    group(2, [m0b, s0b])
    group(3, [d0a, swap(d0a)])
    group(4, [d0b, swap(d0b)])
    group(5, [m1a, swap(m1a)])
    r_own, r0a, r0b = close(0), close(1), close(2)
    group(6, [m1b, swap(m1b)])
    group(7, [m1c, swap(m1c)])
    rda, rdb = close(3), close(4)
    columns = state["column"]
    summed = columns
    for s in range(1, chips):
        summed += lax.ppermute(columns, "tensor", [(i, i ^ s) for i in range(chips)])
    r1a, r1b, r1c = close(5), close(6), close(7)

    join = functools.partial(jnp.concatenate, axis=1)
    same = r_own[0] + join([r0a[0], r0b[0]]) + join([rda[1], rdb[1]]) + join([r1a[1], r1b[1], r1c[1]])
    other = r_own[1] + join([r0a[1], r0b[1]]) + join([rda[0], rdb[0]]) + join([r1a[0], r1b[0], r1c[0]])
    row = jnp.where(core == 0, join([same, other]), join([other, same]))
    row_residual = row.T * CHECK_BLOCK ** (-0.5)
    col_residual = summed[0] * total_rows ** (-0.5)
    return state["out"], row_residual, col_residual


def plain(hidden, hidden_check, down_weight, weight_check):
    total_rows = hidden.shape[0] * lax.axis_size("dp")
    gathered = lax.all_gather(hidden, "dp", axis=0, tiled=True)
    check_part = jnp.dot(gathered, weight_check, preferred_element_type=jnp.float32)
    check_rows = jnp.dot(hidden_check, down_weight, preferred_element_type=jnp.float32)
    partial_value = jnp.dot(gathered, down_weight, preferred_element_type=jnp.float32)
    differ_part = check_part - partial_value.reshape(total_rows, -1, CHECK_BLOCK).sum(-1)
    column_total = lax.psum(check_rows.sum(0) - partial_value.sum(0), "tensor")
    summed = lax.psum_scatter(partial_value, "tensor", scatter_dimension=0, tiled=True)
    row_differ = lax.psum_scatter(differ_part, "tensor", scatter_dimension=0, tiled=True)
    return (
        summed.astype(jnp.bfloat16),
        row_differ * CHECK_BLOCK ** (-0.5),
        column_total * total_rows ** (-0.5),
    )


def solution(mesh):
    placed = (P("dp", "tensor"), P(None, "tensor"), P("tensor", "dp"), P("tensor", "dp"))
    shape = dict(mesh.shape)
    square = shape["tensor"] == 4 and shape["dp"] == 2 * shape["tensor"]
    body = functools.partial(planned, shape) if square else plain
    return jax.shard_map(
        body,
        mesh=mesh,
        in_specs=placed,
        out_specs=(P("tensor", "dp"), P("tensor", "dp"), P("dp")),
        check_vma=False,
    )
```
